512 devices in a mesh: row: 16 (over y_lo, x, core), col: 32 (over z, y_hi).
Axes of the slice: x: 4, y: 4 (y_hi: 2, y_lo: 2; y = y_hi * 2 + y_lo), z: 16, core: 2. Of those that a mesh axis runs over, the one named last changes fastest.
Arguments:
- amplitudes: bfloat16 [32768, 16384], P('row', 'col'), may hold values from -6 to 6
- integrals: bfloat16 [16384, 2048], P('col'), may hold values from -0.125 to 0.125
- pair_index: int32 [32768], P('row'), may hold values from 0 to 39999, as said below
- partner: int32 [32768], P('row'), may hold values from 0 to 32767, as said below
- occ_energy: float32 [200], replicated, may hold values from -1 to -0.3
- vir_energy: float32 [2000], replicated, may hold values from 0.05 to 1
Outputs:
- increment: bfloat16 [32768, 16384], P('row', 'col')
The draws below stay inside these ranges and needn't reach their ends.
Inputs may be any that keep to these rules, and one draw needn't show every extreme that they name: `pair_index`: rows 0 and 1 hold the pairs (199, 199) and (0, 0); otherwise i and j are independent and uniform over 0 to 199. partner is an involution; partner[k] lies in row block (k // 2048) XOR (8), and pair_index[partner[k]] is pair_index[k] with i and j exchanged.
All inputs are finite; a program needn't handle non-finite values.
Results may differ from the reference program's by a relative error of at most 0.001.
Values may be sent and summed in bfloat16 or wider, within the bound.
A program may use at most 128 MiB of HBM per device.

```python
import jax
import jax.numpy as jnp
from jax import lax

NOCC = 200
NV = 2000
STOPS = 4
IJ_DEV = 2048
BLK = 512
IJ = 32768
AB = 16384
N_COL = 32


def joint_pairs(key):
    base = jax.random.fold_in(key, 7)
    key_first, key_second, key_perm = jax.random.split(base, 3)
    half_rows = IJ // 2
    block_count = half_rows // IJ_DEV
    first = jax.random.randint(key_first, (half_rows,), 0, NOCC)
    second = jax.random.randint(key_second, (half_rows,), 0, NOCC)
    first = first.at[0].set(NOCC - 1).at[1].set(0)
    second = second.at[0].set(NOCC - 1).at[1].set(0)
    lower = first * NOCC + second
    upper_source = (second * NOCC + first).reshape(block_count, IJ_DEV)
    perm_keys = jax.random.split(key_perm, block_count)
    placed = jax.vmap(lambda k: jax.random.permutation(k, IJ_DEV))(perm_keys).astype(jnp.int32)
    inverse = jnp.argsort(placed, axis=1, stable=True).astype(jnp.int32)
    upper = jnp.take_along_axis(upper_source, inverse, axis=1).reshape(-1)
    block_start = (jnp.arange(block_count, dtype=jnp.int32) * IJ_DEV)[:, None]
    lower_partner = (half_rows + block_start + placed).reshape(-1)
    upper_partner = (block_start + inverse).reshape(-1)
    pair_values = jnp.concatenate([lower, upper]).astype(jnp.int32)
    partner_values = jnp.concatenate([lower_partner, upper_partner]).astype(jnp.int32)
    return (pair_values, partner_values)


def draw_pair_index(key, part):
    return joint_pairs(key)[0]


def draw_partner(key, part):
    return joint_pairs(key)[1]


def steps_of(key, extent, shards, least, top_value):
    def one(dim, blocks):
        steps = jax.random.uniform(jax.random.fold_in(jax.random.fold_in(key, 6), dim), (blocks,), jnp.float32, least / len(shards), top_value / len(shards))
        return jnp.repeat(jnp.exp(steps), extent[dim] // blocks).reshape((-1,) + (1,) * (len(extent) - dim - 1))

    gain = one(*shards[0])
    for cut in shards[1:]:
        gain = gain * one(*cut)
    return gain


def normal_values(own_key, dims, spread, most, cuts=(), kind=jnp.bfloat16):
    result = spread * jax.random.normal(own_key, dims, jnp.float32)
    if cuts:
        result = result * steps_of(own_key, dims, cuts, -0.22, 0.18)
    return jnp.clip(result, -most, most).astype(kind)


def setup_inputs(seed: int = 0) -> dict:
    key_list = jax.random.split(jax.random.key(seed), 7)
    amplitudes = normal_values(key_list[0], (IJ, AB), 1.0, 6.0, ((0, 16), (1, 32)))
    integrals = normal_values(key_list[1], (AB, STOPS * BLK), (STOPS * BLK) ** -0.5, 0.125, ((0, 32),))
    pair_index = draw_pair_index(jax.random.fold_in(key_list[6], 71), 0)
    partner = draw_partner(jax.random.fold_in(key_list[6], 71), 0)
    occ_energy = jnp.clip(jax.random.uniform(key_list[4], (NOCC,), jnp.float32, -1.0, -0.3), -1.0, -0.3)
    vir_energy = jnp.clip(jax.random.uniform(key_list[5], (NV,), jnp.float32, 0.05, 1.0), 0.05, 1.0)
    return {"amplitudes": amplitudes, "integrals": integrals, "pair_index": pair_index, "partner": partner, "occ_energy": occ_energy, "vir_energy": vir_energy}


def mirror_pairs(values):
    pair_width = values.shape[1]
    parity = (jnp.arange(pair_width, dtype=jnp.int32) % 2) == 0
    return jnp.where(parity[None, :], jnp.roll(values, -1, axis=1), jnp.roll(values, 1, axis=1))


def reference(amplitudes, integrals, pair_index, partner, occ_energy, vir_energy):
    ij_all = amplitudes.shape[0]
    pair_width = BLK
    occ_sum = occ_energy[pair_index // NOCC] + occ_energy[pair_index % NOCC]

    def one_block(block_index):
        running = jnp.zeros((ij_all, pair_width), jnp.float32)
        for stop_index in range(STOPS):
            source = ((block_index - stop_index) % N_COL).astype(jnp.int32)
            tile = lax.dynamic_slice_in_dim(amplitudes, source * pair_width, pair_width, 1)
            piece = lax.dynamic_slice(integrals, (source * pair_width, jnp.int32(stop_index * pair_width)), (pair_width, pair_width))
            running = running + jnp.dot(tile, piece, preferred_element_type=jnp.float32)
        opposite = mirror_pairs(jnp.take(running, partner, axis=0))
        global_pair = block_index * pair_width + jnp.arange(pair_width, dtype=jnp.int32)
        unordered = global_pair // 2
        vir_sum = vir_energy[unordered // NV] + vir_energy[unordered % NV]
        denom = vir_sum[None, :] - occ_sum[:, None]
        return ((running + opposite) / denom).astype(jnp.bfloat16)

    stacked = lax.map(one_block, jnp.arange(N_COL, dtype=jnp.int32))
    return jnp.transpose(stacked, (1, 0, 2)).reshape(ij_all, N_COL * pair_width)
```

```python
import functools

import jax
import jax.numpy as jnp
from jax import lax
from jax.experimental import pallas as pl
from jax.experimental.pallas import tpu as pltpu
from jax.sharding import PartitionSpec as P

NOCC = 200
NV = 2000
STOPS = 4
CHUNK = 128
LEVELS = 32767.0
MESH = pl.DeviceIdType.MESH


def table_lookup(table, positions):
    slots = jnp.arange(table.shape[0], dtype=jnp.int32)
    return jnp.sum(jnp.where(positions[:, None] == slots[None, :], table[None, :], 0.0), axis=1)


def encode(values, code_ref, scale_ref):
    top = jnp.maximum(jnp.max(jnp.abs(values), axis=0, keepdims=True), 1e-30)
    code = jnp.round(values * (LEVELS / top))
    code_ref[...] = code.astype(jnp.int32).astype(jnp.int16)
    scale_ref[...] = top * (1.0 / LEVELS)


def decode(code_ref, scale_ref):
    return code_ref[...].astype(jnp.int32).astype(jnp.float32) * scale_ref[...]


def kernel(
    chunks,
    width,
    row_half,
    col_count,
    amp,
    integ,
    slot_row,
    slot_col,
    occ_row,
    vir_row,
    out,
    weights,
    rows_send,
    rows_recv,
    part0,
    part1,
    part2,
    occ_chunk,
    code_send,
    code_recv,
    scale_send,
    scale_recv,
    inc_send,
    inc_all,
    rows_ssem,
    rows_rsem,
    code_ssem,
    code_rsem,
    scale_ssem,
    scale_rsem,
    inc_ssem,
    inc_rsem,
):
    row = lax.axis_index("row")
    col = lax.axis_index("col")
    upper = row // row_half
    odd = col % 2
    mine = (upper + odd) % 2
    half = chunks * CHUNK
    row_count = 2 * half
    partner = (row + row_half) % (2 * row_half)
    col_up = (col + 2) % col_count
    col_down = (col + col_count - 2) % col_count
    col_flip = col + 1 - 2 * odd

    barrier = pltpu.get_barrier_semaphore()
    for peer in ((partner, col), (partner, col_flip), (row, col_up), (row, col_down)):
        pl.semaphore_signal(barrier, inc=1, device_id=peer, device_id_type=MESH)

    def send_rows(c):
        return pltpu.make_async_remote_copy(
            src_ref=rows_send.at[c],
            dst_ref=rows_recv.at[c],
            send_sem=rows_ssem.at[c],
            recv_sem=rows_rsem.at[c],
            device_id=(partner, col),
            device_id_type=MESH,
        )

    def send_code(stream, c):
        peer = ((row, col_up), (partner, col_flip), (row, col_up))[stream]
        data = pltpu.make_async_remote_copy(
            src_ref=code_send.at[stream, c],
            dst_ref=code_recv.at[stream, c],
            send_sem=code_ssem.at[stream, c],
            recv_sem=code_rsem.at[stream, c],
            device_id=peer,
            device_id_type=MESH,
        )
        scale = pltpu.make_async_remote_copy(
            src_ref=scale_send.at[stream, c],
            dst_ref=scale_recv.at[stream, c],
            send_sem=scale_ssem.at[stream, c],
            recv_sem=scale_rsem.at[stream, c],
            device_id=peer,
            device_id_type=MESH,
        )
        return data, scale

    def send_inc(c):
        return pltpu.make_async_remote_copy(
            src_ref=inc_send.at[c],
            dst_ref=inc_all.at[c, pl.ds(CHUNK, CHUNK)],
            send_sem=inc_ssem.at[c],
            recv_sem=inc_rsem.at[c],
            device_id=(partner, col),
            device_id_type=MESH,
        )

    def push(stream, c, values):
        encode(values, code_send.at[stream, c], scale_send.at[stream, c])
        for copy in send_code(stream, c):
            copy.start()

    def arrived(stream, c):
        for copy in send_code(stream, c):
            copy.wait_recv()
        return decode(code_recv.at[stream, c], scale_recv.at[stream, c])

    def picks(base):
        places = base + lax.broadcasted_iota(jnp.int32, (CHUNK, row_count), 0)
        return slot_row[...] == places

    def own_rows(choice):
        one_hot = jnp.where(choice, 1.0, 0.0).astype(jnp.bfloat16)
        return jnp.dot(one_hot, amp[...], preferred_element_type=jnp.float32).astype(jnp.bfloat16)

    rows_send[0] = own_rows(picks((1 - mine) * half))
    pl.semaphore_wait(barrier, 4)
    send_rows(0).start()

    @pl.loop(1, chunks)
    def _(c):
        rows_send[c] = own_rows(picks((1 - mine) * half + c * CHUNK))
        send_rows(c).start()

    out[...] = jnp.zeros_like(out)
    tile = 256
    left = lax.broadcasted_iota(jnp.int32, (tile, tile), 0)
    right = lax.broadcasted_iota(jnp.int32, (tile, tile), 1)
    step = 1 - 2 * (right % 2)
    for side in range(2):
        moved = upper if side == 0 else 1 - upper
        swap = jnp.where(left == right + moved * step, 1.0, 0.0).astype(jnp.bfloat16)
        for t in range(STOPS * width // tile):
            cols = pl.ds(t * tile, tile)
            weights[side, :, cols] = jnp.dot(
                integ[:, cols], swap, preferred_element_type=jnp.float32
            ).astype(jnp.bfloat16)

    even_lane = lax.broadcasted_iota(jnp.int32, (CHUNK, width), 1) % 2 == 0
    lanes = lax.broadcasted_iota(jnp.int32, (row_count, CHUNK), 1)
    is_even = (1 - odd).astype(jnp.float32)
    is_odd = odd.astype(jnp.float32)
    is_upper = lax.broadcasted_iota(jnp.int32, (CHUNK, width), 1) * 0 + upper > 0

    @pl.loop(0, chunks + 4)
    def _(t):
        @pl.when(t < chunks)
        def _():
            choice = picks(mine * half + t * CHUNK)
            occ_chunk[t] = jnp.sum(jnp.where(choice, occ_row[...], 0.0), axis=1, keepdims=True)
            own = own_rows(choice)
            send_rows(t).wait_recv()
            other = rows_recv[t]

            def product(s):
                cols = pl.ds(s * width, width)
                return jnp.dot(own, weights[0, :, cols], preferred_element_type=jnp.float32) + jnp.dot(
                    other, weights[1, :, cols], preferred_element_type=jnp.float32
                )

            push(0, t, product(3))
            part1[t] = product(1)
            part2[t] = product(2)
            part0[t] = product(0)

        @pl.when((t >= 1) & (t < chunks + 1))
        def _():
            c = t - 1
            push(1, c, part1[c] + arrived(0, c))

        @pl.when((t >= 2) & (t < chunks + 2))
        def _():
            c = t - 2
            across = arrived(1, c)
            push(2, c, part2[c] + across * is_even)
            part0[c] = part0[c] + across * is_odd

        @pl.when((t >= 3) & (t < chunks + 3))
        def _():
            c = t - 3
            total = part0[c] + arrived(2, c)
            plain = total / (vir_row[...] - occ_chunk[c])
            mirrored = jnp.where(
                even_lane,
                pltpu.roll(plain, width - 1, axis=1),
                pltpu.roll(plain, 1, axis=1),
            )
            inc_send[c] = jnp.where(is_upper, plain, mirrored).astype(jnp.bfloat16)
            send_inc(c).start()
            inc_all[c, pl.ds(0, CHUNK)] = jnp.where(is_upper, mirrored, plain).astype(jnp.bfloat16)

        @pl.when(t >= 4)
        def _():
            c = t - 4
            send_inc(c).wait_recv()
            values = inc_all[c]
            group = min(512, row_count)
            for j in range(row_count // group):
                rows = pl.ds(j * group, group)
                at = slot_col[rows, :]
                lane = lanes[j * group : (j + 1) * group]
                near = jnp.where(at == lane + (mine * half + c * CHUNK), 1.0, 0.0)
                far = jnp.where(at == lane + ((1 - mine) * half + c * CHUNK), 1.0, 0.0)
                one_hot = jnp.concatenate([near, far], axis=1).astype(jnp.bfloat16)
                found = jnp.dot(one_hot, values, preferred_element_type=jnp.float32)
                out[rows, :] = out[rows, :] + found.astype(jnp.bfloat16)

    @pl.loop(0, chunks)
    def _(c):
        send_rows(c).wait_send()
        for stream in range(3):
            for copy in send_code(stream, c):
                copy.wait_send()
        send_inc(c).wait_send()


def shards(amplitudes, integrals, pair_index, partner, occ_energy, vir_energy):
    row_count, width = amplitudes.shape
    row_half = lax.axis_size("row") // 2
    col_count = lax.axis_size("col")
    chunks = row_count // 2 // CHUNK
    upper = lax.axis_index("row") // row_half
    own_place = jnp.arange(row_count, dtype=jnp.int32)
    slot = jnp.where(upper == 0, own_place, partner % row_count)
    occ_sum = table_lookup(occ_energy, pair_index // NOCC) + table_lookup(
        occ_energy, pair_index % NOCC
    )
    global_pair = lax.axis_index("col") * width + jnp.arange(width, dtype=jnp.int32)
    unordered = global_pair // 2
    vir_sum = table_lookup(vir_energy, unordered // NV) + table_lookup(vir_energy, unordered % NV)
    vmem = pl.BlockSpec(memory_space=pltpu.VMEM)
    dma = pltpu.SemaphoreType.DMA
    return pl.pallas_call(
        functools.partial(kernel, chunks, width, row_half, col_count),
        out_shape=jax.ShapeDtypeStruct((row_count, width), jnp.bfloat16),
        in_specs=[vmem] * 6,
        out_specs=vmem,
        scratch_shapes=[
            pltpu.VMEM((2, width, STOPS * width), jnp.bfloat16),
            pltpu.VMEM((chunks, CHUNK, width), jnp.bfloat16),
            pltpu.VMEM((chunks, CHUNK, width), jnp.bfloat16),
            pltpu.VMEM((chunks, CHUNK, width), jnp.float32),
            pltpu.VMEM((chunks, CHUNK, width), jnp.float32),
            pltpu.VMEM((chunks, CHUNK, width), jnp.float32),
            pltpu.VMEM((chunks, CHUNK, 1), jnp.float32),
            pltpu.VMEM((3, chunks, CHUNK, width), jnp.int16),
            pltpu.VMEM((3, chunks, CHUNK, width), jnp.int16),
            pltpu.VMEM((3, chunks, 1, width), jnp.float32),
            pltpu.VMEM((3, chunks, 1, width), jnp.float32),
            pltpu.VMEM((chunks, CHUNK, width), jnp.bfloat16),
            pltpu.VMEM((chunks, 2 * CHUNK, width), jnp.bfloat16),
            dma((chunks,)),
            dma((chunks,)),
            dma((3, chunks)),
            dma((3, chunks)),
            dma((3, chunks)),
            dma((3, chunks)),
            dma((chunks,)),
            dma((chunks,)),
        ],
        compiler_params=pltpu.CompilerParams(
            collective_id=0, has_side_effects=True, vmem_limit_bytes=56 * 1024 * 1024
        ),
    )(
        amplitudes,
        integrals,
        slot[None, :],
        jnp.broadcast_to(slot[:, None], (row_count, CHUNK)),
        occ_sum[None, :],
        vir_sum[None, :],
    )


def solution(mesh):
    in_specs = (P("row", "col"), P("col", None), P("row"), P("row"), P(), P())
    out_specs = P("row", "col")
    return jax.shard_map(shards, mesh=mesh, in_specs=in_specs, out_specs=out_specs, check_vma=False)
```

```python
import functools

import jax
import jax.numpy as jnp
from jax import lax
from jax.experimental import pallas as pl
from jax.experimental.pallas import tpu as pltpu
from jax.sharding import PartitionSpec as P

NOCC = 200
NV = 2000
STOPS = 4
CHUNK = 128
LAGS = (2, 4, 6, 8)
ZA, YA, ZB, YB = range(4)
LEVELS = 32767.0
MESH = pl.DeviceIdType.MESH
F32 = jnp.float32
BF16 = jnp.bfloat16


def iota(shape, dim):
    return lax.broadcasted_iota(jnp.int32, shape, dim)


def encode(values, code_ref, scale_ref):
    top = jnp.maximum(jnp.max(jnp.abs(values), axis=0, keepdims=True), 1e-30)
    code = jnp.round(values * (LEVELS / top))
    code_ref[...] = code.astype(jnp.int32).astype(jnp.int16)
    scale_ref[...] = top * (1.0 / LEVELS)


def decode(code_ref, scale_ref):
    return code_ref[...].astype(jnp.int32).astype(F32) * scale_ref[...]


def lookup(table, position):
    slots = iota((position.shape[0], table.shape[1]), 1).astype(F32)
    return jnp.sum(jnp.where(slots == position, table, 0.0), axis=1, keepdims=True)


def pair_sum(table, base, position):
    first = jnp.floor((position + 0.5) * (1.0 / base))
    return lookup(table, first) + lookup(table, position - first * base)


def place(slot_ref, inc, first, rows):
    at = slot_ref[rows, :]
    lane = iota(at.shape, 1)
    near = jnp.where(at == lane + first[0], 1.0, 0.0)
    far = jnp.where(at == lane + first[1], 1.0, 0.0)
    one_hot = jnp.concatenate([near, far], axis=1).astype(BF16)
    return jnp.dot(one_hot, inc, preferred_element_type=F32).astype(BF16)


def kernel(
    chunks,
    width,
    row_half,
    col_count,
    amp_hbm,
    integ_hbm,
    partner_hbm,
    pair_hbm,
    occ_hbm,
    vir_hbm,
    acc,
    slot_col,
    partner_row,
    pair_row,
    occ_table,
    vir_table,
    amp,
    integ,
    mirror,
    slot_row,
    pair_f,
    vir_row,
    rows_send,
    rows_all,
    part,
    total,
    occ_chunk,
    code_send,
    code_recv,
    scale_send,
    scale_recv,
    inc_send,
    inc_all,
    load_sem,
    rows_ssem,
    rows_rsem,
    code_ssem,
    code_rsem,
    scale_ssem,
    scale_rsem,
    inc_ssem,
    inc_rsem,
):
    row = lax.axis_index("row")
    col = lax.axis_index("col")
    upper = row // row_half
    odd = col % 2
    mine = (upper + odd) % 2
    half = chunks * CHUNK
    row_count = 2 * half
    partner = (row + row_half) % (2 * row_half)
    col_up = (col + 2) % col_count
    col_down = (col + col_count - 2) % col_count
    col_flip = col + 1 - 2 * odd

    loads = [
        pltpu.make_async_copy(source, target, load_sem.at[i])
        for i, (source, target) in enumerate(
            (
                (partner_hbm, partner_row),
                (amp_hbm, amp),
                (pair_hbm, pair_row),
                (occ_hbm, occ_table),
                (vir_hbm, vir_table),
                (integ_hbm, integ),
            )
        )
    ]
    for load in loads[:-1]:
        load.start()

    barrier = pltpu.get_barrier_semaphore()
    for peer in ((partner, col), (partner, col_flip), (row, col_up), (row, col_down)):
        pl.semaphore_signal(barrier, inc=1, device_id=peer, device_id_type=MESH)

    def send_rows(c, slot):
        return pltpu.make_async_remote_copy(
            src_ref=rows_send.at[c],
            dst_ref=rows_all.at[slot, c],
            send_sem=rows_ssem.at[c],
            recv_sem=rows_rsem.at[c],
            device_id=(partner, col),
            device_id_type=MESH,
        )

    def send_code(stream, c):
        peer = (row, col_up) if stream in (ZA, ZB) else (partner, col_flip)
        data = pltpu.make_async_remote_copy(
            src_ref=code_send.at[stream, c],
            dst_ref=code_recv.at[stream, c],
            send_sem=code_ssem.at[stream, c],
            recv_sem=code_rsem.at[stream, c],
            device_id=peer,
            device_id_type=MESH,
        )
        scale = pltpu.make_async_remote_copy(
            src_ref=scale_send.at[stream, c],
            dst_ref=scale_recv.at[stream, c],
            send_sem=scale_ssem.at[stream, c],
            recv_sem=scale_rsem.at[stream, c],
            device_id=peer,
            device_id_type=MESH,
        )
        return data, scale

    def send_inc(c):
        return pltpu.make_async_remote_copy(
            src_ref=inc_send.at[c],
            dst_ref=inc_all.at[c, pl.ds(CHUNK, CHUNK)],
            send_sem=inc_ssem.at[c],
            recv_sem=inc_rsem.at[c],
            device_id=(partner, col),
            device_id_type=MESH,
        )

    def push(stream, c, values):
        encode(values, code_send.at[stream, c], scale_send.at[stream, c])
        for copy in send_code(stream, c):
            copy.start()

    def arrived(stream, c):
        for copy in send_code(stream, c):
            copy.wait_recv()
        return decode(code_recv.at[stream, c], scale_recv.at[stream, c])

    def picks(base):
        return slot_row[...] == base + iota((CHUNK, row_count), 0)

    def own_rows(choice):
        one_hot = jnp.where(choice, 1.0, 0.0).astype(BF16)
        return jnp.dot(one_hot, amp[...], preferred_element_type=F32).astype(BF16)

    loads[0].wait()
    slot_row[...] = jnp.where(
        iota((1, row_count), 1) * 0 + upper > 0,
        partner_row[...] - partner * row_count,
        iota((1, row_count), 1),
    )
    loads[1].wait()
    loads[-1].start()
    rows_send[0] = own_rows(picks((1 - mine) * half))
    pl.semaphore_wait(barrier, 4)
    send_rows(0, upper).start()

    @pl.loop(1, chunks)
    def _(c):
        rows_send[c] = own_rows(picks((1 - mine) * half + c * CHUNK))
        send_rows(c, upper).start()

    for load in loads[2:]:
        load.wait()
    tile = 256
    right = iota((tile, tile), 1)
    swap = jnp.where(iota((tile, tile), 0) == right + 1 - 2 * (right % 2), 1.0, 0.0).astype(BF16)
    for t in range(STOPS * width // tile):
        cols = pl.ds(t * tile, tile)
        mirror[:, cols] = jnp.dot(integ[:, cols], swap, preferred_element_type=F32).astype(BF16)
    pair_f[...] = pair_row[...].astype(F32)

    even_lane = iota((CHUNK, width), 1) % 2 == 0
    is_even = odd == 0
    is_odd = odd == 1
    is_upper = iota((CHUNK, width), 1) * 0 + upper > 0

    def first_hop(c):
        choice = picks(mine * half + c * CHUNK)
        rows_all[upper, c] = own_rows(choice)
        send_rows(c, 1 - upper).wait_recv()
        low = rows_all[0, c]
        high = rows_all[1, c]

        def product(s):
            cols = pl.ds(s * width, width)
            return jnp.dot(low, integ[:, cols], preferred_element_type=F32) + jnp.dot(
                high, mirror[:, cols], preferred_element_type=F32
            )

        for s in range(STOPS):
            part[s, c] = product(s)
        pair = jnp.sum(jnp.where(choice, pair_f[...], 0.0), axis=1, keepdims=True)
        occ_chunk[c] = pair_sum(occ_table[...], NOCC, pair)
        first_kind = c % 2 == 0

        @pl.when(is_odd)
        def _():
            push(ZA, c, part[3, c])

        @pl.when(is_odd & ~first_kind)
        def _():
            push(YB, c, part[2, c])

        @pl.when(is_even & first_kind)
        def _():
            push(YA, c, part[3, c])
            push(YB, c, part[1, c])

    def second_hop(c):
        first_kind = c % 2 == 0

        @pl.when(is_odd)
        def _():
            push(YA, c, part[1, c] + arrived(ZA, c))

        @pl.when(is_odd & first_kind)
        def _():
            push(ZB, c, part[2, c] + arrived(YA, c))

        @pl.when(is_even & ~first_kind)
        def _():
            push(ZB, c, part[3, c] + arrived(YB, c))

    def third_hop(c):
        first_kind = c % 2 == 0

        @pl.when(is_even & ~first_kind)
        def _():
            push(YA, c, part[1, c] + arrived(ZB, c))

        @pl.when(is_even)
        def _():
            push(ZA, c, part[2, c] + arrived(YA, c))

    def finish(c):
        first_kind = c % 2 == 0

        @pl.when(is_even)
        def _():
            total[...] = part[0, c] + arrived(ZA, c)

        @pl.when(is_odd & first_kind)
        def _():
            total[...] = part[0, c] + arrived(ZB, c) + arrived(YB, c)

        @pl.when(is_odd & ~first_kind)
        def _():
            total[...] = part[0, c] + arrived(YA, c)

        plain = total[...] / (vir_row[...] - occ_chunk[c])
        mirrored = jnp.where(
            even_lane,
            pltpu.roll(plain, width - 1, axis=1),
            pltpu.roll(plain, 1, axis=1),
        )
        inc_send[c] = jnp.where(is_upper, plain, mirrored).astype(BF16)
        send_inc(c).start()
        inc_all[c, pl.ds(0, CHUNK)] = jnp.where(is_upper, mirrored, plain).astype(BF16)

    def spread(c):
        send_inc(c).wait_recv()
        values = inc_all[c]
        first = (mine * half + c * CHUNK, (1 - mine) * half + c * CHUNK)
        group = min(512, row_count)
        for j in range(row_count // group):
            rows = pl.ds(j * group, group)
            acc[rows, :] = acc[rows, :] + place(slot_col, values, first, rows)

    @pl.loop(0, chunks + LAGS[3])
    def _(t):
        @pl.when(t < chunks)
        def _():
            first_hop(t)

        @pl.when((t >= LAGS[0]) & (t < chunks + LAGS[0]))
        def _():
            second_hop(t - LAGS[0])

        @pl.when((t >= LAGS[1]) & (t < chunks + LAGS[1]))
        def _():
            third_hop(t - LAGS[1])

        @pl.when(t == LAGS[1])
        def _():
            pairs = width // 2
            unordered = col * pairs + iota((pairs, 1), 0)
            values = pair_sum(vir_table[...], NV, unordered.astype(F32))
            same = iota((pairs, width), 1) // 2 == iota((pairs, width), 0)
            vir_row[...] = jnp.sum(jnp.where(same, values, 0.0), axis=0, keepdims=True)
            for j in range(row_count // CHUNK):
                rows = pl.ds(j * CHUNK, CHUNK)
                block = jnp.broadcast_to(slot_row[:, rows], (CHUNK, CHUNK))
                slot_col[rows, :] = block.T
            acc[...] = jnp.zeros_like(acc)

        @pl.when((t >= LAGS[2]) & (t < chunks + LAGS[2]))
        def _():
            finish(t - LAGS[2])

        @pl.when(t >= LAGS[3])
        def _():
            spread(t - LAGS[3])

    @pl.loop(0, chunks)
    def _(c):
        first_kind = c % 2 == 0
        send_rows(c, upper).wait_send()
        send_inc(c).wait_send()
        for stream in (ZA, YA):
            for copy in send_code(stream, c):
                copy.wait_send()

        @pl.when(is_odd == first_kind)
        def _():
            for copy in send_code(ZB, c):
                copy.wait_send()

        @pl.when(is_even == first_kind)
        def _():
            for copy in send_code(YB, c):
                copy.wait_send()


def shards(amplitudes, integrals, pair_index, partner, occ_energy, vir_energy):
    row_count, width = amplitudes.shape
    row_half = lax.axis_size("row") // 2
    col_count = lax.axis_size("col")
    chunks = row_count // 2 // CHUNK
    dma = pltpu.SemaphoreType.DMA
    return pl.pallas_call(
        functools.partial(kernel, chunks, width, row_half, col_count),
        out_shape=jax.ShapeDtypeStruct((row_count, width), BF16),
        in_specs=[pl.BlockSpec(memory_space=pltpu.HBM)] * 6,
        out_specs=pl.BlockSpec(memory_space=pltpu.VMEM),
        scratch_shapes=[
            pltpu.VMEM((row_count, CHUNK), jnp.int32),
            pltpu.VMEM((1, row_count), jnp.int32),
            pltpu.VMEM((1, row_count), jnp.int32),
            pltpu.VMEM((1, occ_energy.shape[0]), F32),
            pltpu.VMEM((1, vir_energy.shape[0]), F32),
            pltpu.VMEM((row_count, width), BF16),
            pltpu.VMEM((width, STOPS * width), BF16),
            pltpu.VMEM((width, STOPS * width), BF16),
            pltpu.VMEM((1, row_count), jnp.int32),
            pltpu.VMEM((1, row_count), F32),
            pltpu.VMEM((1, width), F32),
            pltpu.VMEM((chunks, CHUNK, width), BF16),
            pltpu.VMEM((2, chunks, CHUNK, width), BF16),
            pltpu.VMEM((STOPS, chunks, CHUNK, width), F32),
            pltpu.VMEM((CHUNK, width), F32),
            pltpu.VMEM((chunks, CHUNK, 1), F32),
            pltpu.VMEM((4, chunks, CHUNK, width), jnp.int16),
            pltpu.VMEM((4, chunks, CHUNK, width), jnp.int16),
            pltpu.VMEM((4, chunks, 1, width), F32),
            pltpu.VMEM((4, chunks, 1, width), F32),
            pltpu.VMEM((chunks, CHUNK, width), BF16),
            pltpu.VMEM((chunks, 2 * CHUNK, width), BF16),
            dma((6,)),
            dma((chunks,)),
            dma((chunks,)),
            dma((4, chunks)),
            dma((4, chunks)),
            dma((4, chunks)),
            dma((4, chunks)),
            dma((chunks,)),
            dma((chunks,)),
        ],
        compiler_params=pltpu.CompilerParams(
            collective_id=0, has_side_effects=True, vmem_limit_bytes=48 * 1024 * 1024
        ),
    )(
        pltpu.with_memory_space_constraint(amplitudes, pltpu.HBM),
        pltpu.with_memory_space_constraint(integrals, pltpu.HBM),
        pltpu.with_memory_space_constraint(partner[None, :], pltpu.HBM),
        pltpu.with_memory_space_constraint(pair_index[None, :], pltpu.HBM),
        pltpu.with_memory_space_constraint(occ_energy[None, :], pltpu.HBM),
        pltpu.with_memory_space_constraint(vir_energy[None, :], pltpu.HBM),
    )


def solution(mesh):
    in_specs = (P("row", "col"), P("col", None), P("row"), P("row"), P(), P())
    out_specs = P("row", "col")
    return jax.shard_map(shards, mesh=mesh, in_specs=in_specs, out_specs=out_specs, check_vma=False)
```

```python
import functools

import jax
import jax.numpy as jnp
from jax import lax
from jax.experimental import pallas as pl
from jax.experimental.pallas import tpu as pltpu
from jax.sharding import PartitionSpec as P

NOCC = 200
NV = 2000
STOPS = 4
CHUNK = 128
PIECE = 64
LAGS = (3, 6, 9, 13)
ZA, YA, ZB, YB = range(4)
LEVELS = 32767.0
MESH = pl.DeviceIdType.MESH
F32 = jnp.float32
BF16 = jnp.bfloat16


def iota(shape, dim):
    return lax.broadcasted_iota(jnp.int32, shape, dim)


def encode(values, code_ref, scale_ref):
    top = jnp.maximum(jnp.max(jnp.abs(values), axis=0, keepdims=True), 1e-30)
    code = jnp.round(values * (LEVELS / top))
    code_ref[...] = code.astype(jnp.int32).astype(jnp.int16)
    scale_ref[...] = top * (1.0 / LEVELS)


def decode(code_ref, scale_ref):
    return code_ref[...].astype(jnp.int32).astype(F32) * scale_ref[...]


def lookup(table, position):
    slots = iota((position.shape[0], table.shape[1]), 1).astype(F32)
    return jnp.sum(jnp.where(slots == position, table, 0.0), axis=1, keepdims=True)


def pair_sum(table, base, position):
    first = jnp.floor((position + 0.5) * (1.0 / base))
    return lookup(table, first) + lookup(table, position - first * base)


def place(slot_ref, inc, first, rows):
    at = slot_ref[rows, :]
    lane = iota(at.shape, 1)
    near = jnp.where(at == lane + first[0], 1.0, 0.0)
    far = jnp.where(at == lane + first[1], 1.0, 0.0)
    one_hot = jnp.concatenate([near, far], axis=1).astype(BF16)
    return jnp.dot(one_hot, inc, preferred_element_type=F32).astype(BF16)


def kernel(
    chunks,
    width,
    row_half,
    col_count,
    amp_hbm,
    integ_hbm,
    partner_hbm,
    pair_hbm,
    occ_hbm,
    vir_hbm,
    acc,
    slot_col,
    partner_row,
    pair_row,
    occ_table,
    vir_table,
    amp,
    integ,
    mirror,
    slot_row,
    pair_f,
    vir_row,
    rows_send,
    rows_all,
    part,
    total,
    occ_chunk,
    code_send,
    code_recv,
    scale_send,
    scale_recv,
    inc_send,
    inc_all,
    load_sem,
    rows_ssem,
    rows_rsem,
    code_ssem,
    code_rsem,
    scale_ssem,
    scale_rsem,
    inc_ssem,
    inc_rsem,
):
    row = lax.axis_index("row")
    col = lax.axis_index("col")
    upper = row // row_half
    odd = col % 2
    mine = (upper + odd) % 2
    half = chunks * CHUNK
    cuts = CHUNK // PIECE
    pieces = chunks * cuts
    row_count = 2 * half
    partner = (row + row_half) % (2 * row_half)
    col_up = (col + 2) % col_count
    col_down = (col + col_count - 2) % col_count
    col_flip = col + 1 - 2 * odd

    loads = [
        pltpu.make_async_copy(source, target, load_sem.at[i])
        for i, (source, target) in enumerate(
            (
                (partner_hbm, partner_row),
                (amp_hbm, amp),
                (pair_hbm, pair_row),
                (occ_hbm, occ_table),
                (vir_hbm, vir_table),
                (integ_hbm, integ),
            )
        )
    ]
    for load in loads[:-1]:
        load.start()

    barrier = pltpu.get_barrier_semaphore()
    for peer in ((partner, col), (partner, col_flip), (row, col_up), (row, col_down)):
        pl.semaphore_signal(barrier, inc=1, device_id=peer, device_id_type=MESH)

    def send_rows(c, slot):
        return pltpu.make_async_remote_copy(
            src_ref=rows_send.at[c],
            dst_ref=rows_all.at[slot, c],
            send_sem=rows_ssem.at[c],
            recv_sem=rows_rsem.at[c],
            device_id=(partner, col),
            device_id_type=MESH,
        )

    def send_code(stream, c):
        peer = (row, col_up) if stream in (ZA, ZB) else (partner, col_flip)
        data = pltpu.make_async_remote_copy(
            src_ref=code_send.at[stream, c],
            dst_ref=code_recv.at[stream, c],
            send_sem=code_ssem.at[stream, c],
            recv_sem=code_rsem.at[stream, c],
            device_id=peer,
            device_id_type=MESH,
        )
        scale = pltpu.make_async_remote_copy(
            src_ref=scale_send.at[stream, c],
            dst_ref=scale_recv.at[stream, c],
            send_sem=scale_ssem.at[stream, c],
            recv_sem=scale_rsem.at[stream, c],
            device_id=peer,
            device_id_type=MESH,
        )
        return data, scale

    def send_inc(c):
        return pltpu.make_async_remote_copy(
            src_ref=inc_send.at[c],
            dst_ref=inc_all.at[c // cuts, pl.ds(CHUNK + c % cuts * PIECE, PIECE)],
            send_sem=inc_ssem.at[c],
            recv_sem=inc_rsem.at[c],
            device_id=(partner, col),
            device_id_type=MESH,
        )

    def push(stream, c, values):
        encode(values, code_send.at[stream, c], scale_send.at[stream, c])
        for copy in send_code(stream, c):
            copy.start()

    def arrived(stream, c):
        for copy in send_code(stream, c):
            copy.wait_recv()
        return decode(code_recv.at[stream, c], scale_recv.at[stream, c])

    def picks(base):
        return slot_row[...] == base + iota((CHUNK, row_count), 0)

    def own_rows(choice):
        one_hot = jnp.where(choice, 1.0, 0.0).astype(BF16)
        return jnp.dot(one_hot, amp[...], preferred_element_type=F32).astype(BF16)

    loads[0].wait()
    slot_row[...] = jnp.where(
        iota((1, row_count), 1) * 0 + upper > 0,
        partner_row[...] - partner * row_count,
        iota((1, row_count), 1),
    )
    loads[1].wait()
    loads[-1].start()
    def ready_rows(c):
        found = own_rows(picks((1 - mine) * half + c * CHUNK))
        for p in range(cuts):
            rows_send[c * cuts + p] = found[p * PIECE : (p + 1) * PIECE]

    ready_rows(0)
    pl.semaphore_wait(barrier, 4)
    for p in range(cuts):
        send_rows(p, upper).start()

    @pl.loop(1, chunks)
    def _(c):
        ready_rows(c)
        for p in range(cuts):
            send_rows(c * cuts + p, upper).start()

    for load in loads[2:]:
        load.wait()
    tile = 256
    right = iota((tile, tile), 1)
    swap = jnp.where(iota((tile, tile), 0) == right + 1 - 2 * (right % 2), 1.0, 0.0).astype(BF16)
    for t in range(STOPS * width // tile):
        cols = pl.ds(t * tile, tile)
        mirror[:, cols] = jnp.dot(integ[:, cols], swap, preferred_element_type=F32).astype(BF16)
    pair_f[...] = pair_row[...].astype(F32)

    even_lane = iota((PIECE, width), 1) % 2 == 0
    is_even = odd == 0
    is_odd = odd == 1
    is_upper = iota((PIECE, width), 1) * 0 + upper > 0

    def first_hop(c):
        choice = picks(mine * half + c * CHUNK)
        own = own_rows(choice)
        for p in range(cuts):
            rows_all[upper, c * cuts + p] = own[p * PIECE : (p + 1) * PIECE]
        for p in range(cuts):
            send_rows(c * cuts + p, 1 - upper).wait_recv()
        low = rows_all[0, pl.ds(c * cuts, cuts)].reshape(CHUNK, width)
        high = rows_all[1, pl.ds(c * cuts, cuts)].reshape(CHUNK, width)

        def multiply(s):
            cols = pl.ds(s * width, width)
            product = jnp.dot(low, integ[:, cols], preferred_element_type=F32) + jnp.dot(
                high, mirror[:, cols], preferred_element_type=F32
            )
            for p in range(cuts):
                part[s, c * cuts + p] = product[p * PIECE : (p + 1) * PIECE]

        def push_parts(stream, s, start):
            for p in range(start, cuts, 2):
                push(stream, c * cuts + p, part[s, c * cuts + p])

        multiply(3)

        @pl.when(is_odd)
        def _():
            for p in range(cuts):
                push(ZA, c * cuts + p, part[3, c * cuts + p])

        @pl.when(is_even)
        def _():
            push_parts(YA, 3, 1)

        multiply(1)

        @pl.when(is_even)
        def _():
            push_parts(YB, 1, 1)

        multiply(2)

        @pl.when(is_odd)
        def _():
            push_parts(YB, 2, 0)

        multiply(0)
        pair = jnp.sum(jnp.where(choice, pair_f[...], 0.0), axis=1, keepdims=True)
        occ = pair_sum(occ_table[...], NOCC, pair)
        for p in range(cuts):
            occ_chunk[c * cuts + p] = occ[p * PIECE : (p + 1) * PIECE]

    def second_hop(c):
        first_kind = c % 2 == 1

        @pl.when(is_odd)
        def _():
            push(YA, c, part[1, c] + arrived(ZA, c))

        @pl.when(is_odd & first_kind)
        def _():
            push(ZB, c, part[2, c] + arrived(YA, c))

        @pl.when(is_even & ~first_kind)
        def _():
            push(ZB, c, part[3, c] + arrived(YB, c))

    def third_hop(c):
        first_kind = c % 2 == 1

        @pl.when(is_even & ~first_kind)
        def _():
            push(YA, c, part[1, c] + arrived(ZB, c))

        @pl.when(is_even)
        def _():
            push(ZA, c, part[2, c] + arrived(YA, c))

    def finish(c):
        first_kind = c % 2 == 1

        @pl.when(is_even)
        def _():
            total[...] = part[0, c] + arrived(ZA, c)

        @pl.when(is_odd & first_kind)
        def _():
            total[...] = part[0, c] + arrived(ZB, c) + arrived(YB, c)

        @pl.when(is_odd & ~first_kind)
        def _():
            total[...] = part[0, c] + arrived(YA, c)

        plain = total[...] / (vir_row[...] - occ_chunk[c])
        mirrored = jnp.where(
            even_lane,
            pltpu.roll(plain, width - 1, axis=1),
            pltpu.roll(plain, 1, axis=1),
        )
        inc_send[c] = jnp.where(is_upper, plain, mirrored).astype(BF16)
        send_inc(c).start()
        inc_all[c // cuts, pl.ds(c % cuts * PIECE, PIECE)] = jnp.where(is_upper, mirrored, plain).astype(BF16)

    def spread(c):
        for p in range(cuts):
            send_inc(c * cuts + p).wait_recv()
        values = inc_all[c]
        first = (mine * half + c * CHUNK, (1 - mine) * half + c * CHUNK)
        group = min(512, row_count)
        for j in range(row_count // group):
            rows = pl.ds(j * group, group)
            acc[rows, :] = acc[rows, :] + place(slot_col, values, first, rows)

    def drain(c):
        first_kind = c % 2 == 1
        send_rows(c, upper).wait_send()
        send_inc(c).wait_send()
        for stream in (ZA, YA):
            for copy in send_code(stream, c):
                copy.wait_send()

        @pl.when(is_odd == first_kind)
        def _():
            for copy in send_code(ZB, c):
                copy.wait_send()

        @pl.when(is_even == first_kind)
        def _():
            for copy in send_code(YB, c):
                copy.wait_send()

    @pl.loop(0, pieces + LAGS[3])
    def _(t):
        @pl.when((t % cuts == 0) & (t < pieces))
        def _():
            first_hop(t // cuts)

        @pl.when((t >= LAGS[0]) & (t < pieces + LAGS[0]))
        def _():
            second_hop(t - LAGS[0])

        @pl.when((t >= LAGS[1]) & (t < pieces + LAGS[1]))
        def _():
            third_hop(t - LAGS[1])

        @pl.when(t == LAGS[1])
        def _():
            pairs = width // 2
            unordered = col * pairs + iota((pairs, 1), 0)
            values = pair_sum(vir_table[...], NV, unordered.astype(F32))
            same = iota((pairs, width), 1) // 2 == iota((pairs, width), 0)
            vir_row[...] = jnp.sum(jnp.where(same, values, 0.0), axis=0, keepdims=True)
            for j in range(row_count // CHUNK):
                rows = pl.ds(j * CHUNK, CHUNK)
                block = jnp.broadcast_to(slot_row[:, rows], (CHUNK, CHUNK))
                slot_col[rows, :] = block.T
            acc[...] = jnp.zeros_like(acc)

        @pl.when((t >= LAGS[2]) & (t < pieces + LAGS[2]))
        def _():
            finish(t - LAGS[2])

        @pl.when((t >= LAGS[3]) & ((t - LAGS[3]) % cuts == cuts - 1))
        def _():
            spread((t - LAGS[3]) // cuts)

        @pl.when(t >= LAGS[3])
        def _():
            drain(t - LAGS[3])


def shards(amplitudes, integrals, pair_index, partner, occ_energy, vir_energy):
    row_count, width = amplitudes.shape
    row_half = lax.axis_size("row") // 2
    col_count = lax.axis_size("col")
    chunks = row_count // 2 // CHUNK
    pieces = row_count // 2 // PIECE
    dma = pltpu.SemaphoreType.DMA
    return pl.pallas_call(
        functools.partial(kernel, chunks, width, row_half, col_count),
        out_shape=jax.ShapeDtypeStruct((row_count, width), BF16),
        in_specs=[pl.BlockSpec(memory_space=pltpu.HBM)] * 6,
        out_specs=pl.BlockSpec(memory_space=pltpu.VMEM),
        scratch_shapes=[
            pltpu.VMEM((row_count, CHUNK), jnp.int32),
            pltpu.VMEM((1, row_count), jnp.int32),
            pltpu.VMEM((1, row_count), jnp.int32),
            pltpu.VMEM((1, occ_energy.shape[0]), F32),
            pltpu.VMEM((1, vir_energy.shape[0]), F32),
            pltpu.VMEM((row_count, width), BF16),
            pltpu.VMEM((width, STOPS * width), BF16),
            pltpu.VMEM((width, STOPS * width), BF16),
            pltpu.VMEM((1, row_count), jnp.int32),
            pltpu.VMEM((1, row_count), F32),
            pltpu.VMEM((1, width), F32),
            pltpu.VMEM((pieces, PIECE, width), BF16),
            pltpu.VMEM((2, pieces, PIECE, width), BF16),
            pltpu.VMEM((STOPS, pieces, PIECE, width), F32),
            pltpu.VMEM((PIECE, width), F32),
            pltpu.VMEM((pieces, PIECE, 1), F32),
            pltpu.VMEM((4, pieces, PIECE, width), jnp.int16),
            pltpu.VMEM((4, pieces, PIECE, width), jnp.int16),
            pltpu.VMEM((4, pieces, 1, width), F32),
            pltpu.VMEM((4, pieces, 1, width), F32),
            pltpu.VMEM((pieces, PIECE, width), BF16),
            pltpu.VMEM((chunks, 2 * CHUNK, width), BF16),
            dma((6,)),
            dma((pieces,)),
            dma((pieces,)),
            dma((4, pieces)),
            dma((4, pieces)),
            dma((4, pieces)),
            dma((4, pieces)),
            dma((pieces,)),
            dma((pieces,)),
        ],
        compiler_params=pltpu.CompilerParams(
            collective_id=0, has_side_effects=True, vmem_limit_bytes=48 * 1024 * 1024
        ),
    )(
        pltpu.with_memory_space_constraint(amplitudes, pltpu.HBM),
        pltpu.with_memory_space_constraint(integrals, pltpu.HBM),
        pltpu.with_memory_space_constraint(partner[None, :], pltpu.HBM),
        pltpu.with_memory_space_constraint(pair_index[None, :], pltpu.HBM),
        pltpu.with_memory_space_constraint(occ_energy[None, :], pltpu.HBM),
        pltpu.with_memory_space_constraint(vir_energy[None, :], pltpu.HBM),
    )


def solution(mesh):
    in_specs = (P("row", "col"), P("col", None), P("row"), P("row"), P(), P())
    out_specs = P("row", "col")
    return jax.shard_map(shards, mesh=mesh, in_specs=in_specs, out_specs=out_specs, check_vma=False)
```

```python
import functools

import jax
import jax.numpy as jnp
from jax import lax
from jax.experimental import pallas as pl
from jax.experimental.pallas import tpu as pltpu
from jax.sharding import PartitionSpec as P

NOCC = 200
NV = 2000
STOPS = 4
CHUNK = 128
PIECE = 64
LOADS = 4
LAGS = (3, 6, 9, 13)
ZA, YA, ZB, YB = range(4)
LEVELS = 32767.0
MESH = pl.DeviceIdType.MESH
F32 = jnp.float32
BF16 = jnp.bfloat16


def iota(shape, dim):
    return lax.broadcasted_iota(jnp.int32, shape, dim)


def encode(values, code_ref, scale_ref):
    top = jnp.maximum(jnp.max(jnp.abs(values), axis=0, keepdims=True), 1e-30)
    code = jnp.round(values * (LEVELS / top))
    code_ref[...] = code.astype(jnp.int32).astype(jnp.int16)
    scale_ref[...] = top * (1.0 / LEVELS)


def decode(code_ref, scale_ref):
    return code_ref[...].astype(jnp.int32).astype(F32) * scale_ref[...]


def lookup(table, position):
    slots = iota((position.shape[0], table.shape[1]), 1).astype(F32)
    return jnp.sum(jnp.where(slots == position, table, 0.0), axis=1, keepdims=True)


def pair_sum(table, base, position):
    first = jnp.floor((position + 0.5) * (1.0 / base))
    return lookup(table, first) + lookup(table, position - first * base)


def place(slot_ref, inc, first, rows):
    at = slot_ref[rows, :]
    lane = iota(at.shape, 1)
    near = jnp.where(at == lane + first[0], 1.0, 0.0)
    far = jnp.where(at == lane + first[1], 1.0, 0.0)
    one_hot = jnp.concatenate([near, far], axis=1).astype(BF16)
    return jnp.dot(one_hot, inc, preferred_element_type=F32).astype(BF16)


def kernel(
    chunks,
    width,
    row_half,
    col_count,
    amp_hbm,
    integ_hbm,
    partner_hbm,
    pair_hbm,
    occ_hbm,
    vir_hbm,
    acc,
    slot_col,
    partner_row,
    pair_row,
    occ_table,
    vir_table,
    amp,
    integ,
    mirror,
    slot_row,
    pair_f,
    vir_row,
    rows_send,
    rows_all,
    part,
    total,
    occ_chunk,
    code_send,
    code_recv,
    scale_send,
    scale_recv,
    inc_send,
    inc_all,
    load_sem,
    rows_ssem,
    rows_rsem,
    code_ssem,
    code_rsem,
    scale_ssem,
    scale_rsem,
    inc_ssem,
    inc_rsem,
):
    row = lax.axis_index("row")
    col = lax.axis_index("col")
    upper = row // row_half
    odd = col % 2
    mine = (upper + odd) % 2
    half = chunks * CHUNK
    cuts = CHUNK // PIECE
    pieces = chunks * cuts
    row_count = 2 * half
    partner = (row + row_half) % (2 * row_half)
    col_up = (col + 2) % col_count
    col_down = (col + col_count - 2) % col_count
    col_flip = col + 1 - 2 * odd

    part_rows = row_count // LOADS
    slices = [pl.ds(i * part_rows, part_rows) for i in range(LOADS)]
    moves = [(partner_hbm, partner_row)]
    moves += [(amp_hbm.at[rows], amp.at[rows]) for rows in slices]
    moves += [(pair_hbm, pair_row), (occ_hbm, occ_table), (vir_hbm, vir_table)]
    moves += [(integ_hbm, integ)]
    loads = [
        pltpu.make_async_copy(source, target, load_sem.at[i])
        for i, (source, target) in enumerate(moves)
    ]
    for load in loads[: 1 + LOADS]:
        load.start()

    barrier = pltpu.get_barrier_semaphore()
    for peer in ((partner, col), (partner, col_flip), (row, col_up), (row, col_down)):
        pl.semaphore_signal(barrier, inc=1, device_id=peer, device_id_type=MESH)

    def send_rows(c, slot):
        return pltpu.make_async_remote_copy(
            src_ref=rows_send.at[c],
            dst_ref=rows_all.at[slot, c],
            send_sem=rows_ssem.at[c],
            recv_sem=rows_rsem.at[c],
            device_id=(partner, col),
            device_id_type=MESH,
        )

    def send_code(stream, c):
        peer = (row, col_up) if stream in (ZA, ZB) else (partner, col_flip)
        data = pltpu.make_async_remote_copy(
            src_ref=code_send.at[stream, c],
            dst_ref=code_recv.at[stream, c],
            send_sem=code_ssem.at[stream, c],
            recv_sem=code_rsem.at[stream, c],
            device_id=peer,
            device_id_type=MESH,
        )
        scale = pltpu.make_async_remote_copy(
            src_ref=scale_send.at[stream, c],
            dst_ref=scale_recv.at[stream, c],
            send_sem=scale_ssem.at[stream, c],
            recv_sem=scale_rsem.at[stream, c],
            device_id=peer,
            device_id_type=MESH,
        )
        return scale, data

    def send_inc(c):
        return pltpu.make_async_remote_copy(
            src_ref=inc_send.at[c],
            dst_ref=inc_all.at[c // cuts, pl.ds(CHUNK + c % cuts * PIECE, PIECE)],
            send_sem=inc_ssem.at[c],
            recv_sem=inc_rsem.at[c],
            device_id=(partner, col),
            device_id_type=MESH,
        )

    def push(stream, c, values):
        encode(values, code_send.at[stream, c], scale_send.at[stream, c])
        for copy in send_code(stream, c):
            copy.start()

    def arrived(stream, c):
        for copy in send_code(stream, c):
            copy.wait_recv()
        return decode(code_recv.at[stream, c], scale_recv.at[stream, c])

    def picks(base):
        return slot_row[...] == base + iota((CHUNK, row_count), 0)

    def own_rows(choice):
        one_hot = jnp.where(choice, 1.0, 0.0).astype(BF16)
        return jnp.dot(one_hot, amp[...], preferred_element_type=F32).astype(BF16)

    loads[0].wait()
    slot_row[...] = jnp.where(
        iota((1, row_count), 1) * 0 + upper > 0,
        partner_row[...] - partner * row_count,
        iota((1, row_count), 1),
    )
    for load in loads[1 : 1 + LOADS]:
        load.wait()
    for load in loads[1 + LOADS :]:
        load.start()
    rows_send[0] = own_rows(picks((1 - mine) * half))
    pl.semaphore_wait(barrier, 4)
    send_rows(0, upper).start()

    @pl.loop(1, chunks)
    def _(c):
        rows_send[c] = own_rows(picks((1 - mine) * half + c * CHUNK))
        send_rows(c, upper).start()

    for load in loads[1 + LOADS :]:
        load.wait()
    tile = 256
    right = iota((tile, tile), 1)
    swap = jnp.where(iota((tile, tile), 0) == right + 1 - 2 * (right % 2), 1.0, 0.0).astype(BF16)
    for t in range(STOPS * width // tile):
        cols = pl.ds(t * tile, tile)
        mirror[:, cols] = jnp.dot(integ[:, cols], swap, preferred_element_type=F32).astype(BF16)
    pair_f[...] = pair_row[...].astype(F32)

    even_lane = iota((PIECE, width), 1) % 2 == 0
    is_even = odd == 0
    is_odd = odd == 1
    is_upper = iota((PIECE, width), 1) * 0 + upper > 0

    def first_hop(c):
        choice = picks(mine * half + c * CHUNK)
        rows_all[upper, c] = own_rows(choice)
        send_rows(c, 1 - upper).wait_recv()
        low = rows_all[0, c]
        high = rows_all[1, c]

        def multiply(s):
            cols = pl.ds(s * width, width)
            product = jnp.dot(low, integ[:, cols], preferred_element_type=F32) + jnp.dot(
                high, mirror[:, cols], preferred_element_type=F32
            )
            for p in range(cuts):
                part[s, c * cuts + p] = product[p * PIECE : (p + 1) * PIECE]

        def push_parts(stream, s, start):
            for p in range(start, cuts, 2):
                push(stream, c * cuts + p, part[s, c * cuts + p])

        multiply(3)

        @pl.when(is_odd)
        def _():
            for p in range(cuts):
                push(ZA, c * cuts + p, part[3, c * cuts + p])

        @pl.when(is_even)
        def _():
            push_parts(YA, 3, 1)

        multiply(1)

        @pl.when(is_even)
        def _():
            push_parts(YB, 1, 1)

        multiply(2)

        @pl.when(is_odd)
        def _():
            push_parts(YB, 2, 0)

        multiply(0)
        pair = jnp.sum(jnp.where(choice, pair_f[...], 0.0), axis=1, keepdims=True)
        occ = pair_sum(occ_table[...], NOCC, pair)
        for p in range(cuts):
            occ_chunk[c * cuts + p] = occ[p * PIECE : (p + 1) * PIECE]

    def second_hop(c):
        first_kind = c % 2 == 1

        @pl.when(is_odd)
        def _():
            push(YA, c, part[1, c] + arrived(ZA, c))

        @pl.when(is_odd & first_kind)
        def _():
            push(ZB, c, part[2, c] + arrived(YA, c))

        @pl.when(is_even & ~first_kind)
        def _():
            push(ZB, c, part[3, c] + arrived(YB, c))

    def third_hop(c):
        first_kind = c % 2 == 1

        @pl.when(is_even & ~first_kind)
        def _():
            push(YA, c, part[1, c] + arrived(ZB, c))

        @pl.when(is_even)
        def _():
            push(ZA, c, part[2, c] + arrived(YA, c))

    def finish(c):
        first_kind = c % 2 == 1

        @pl.when(is_even)
        def _():
            total[...] = part[0, c] + arrived(ZA, c)

        @pl.when(is_odd & first_kind)
        def _():
            total[...] = part[0, c] + arrived(ZB, c) + arrived(YB, c)

        @pl.when(is_odd & ~first_kind)
        def _():
            total[...] = part[0, c] + arrived(YA, c)

        plain = total[...] / (vir_row[...] - occ_chunk[c])
        mirrored = jnp.where(
            even_lane,
            pltpu.roll(plain, width - 1, axis=1),
            pltpu.roll(plain, 1, axis=1),
        )
        inc_send[c] = jnp.where(is_upper, plain, mirrored).astype(BF16)
        send_inc(c).start()
        inc_all[c // cuts, pl.ds(c % cuts * PIECE, PIECE)] = jnp.where(is_upper, mirrored, plain).astype(BF16)

    def spread(c):
        for p in range(cuts):
            send_inc(c * cuts + p).wait_recv()
        values = inc_all[c]
        first = (mine * half + c * CHUNK, (1 - mine) * half + c * CHUNK)
        group = min(512, row_count)
        for j in range(row_count // group):
            rows = pl.ds(j * group, group)
            acc[rows, :] = acc[rows, :] + place(slot_col, values, first, rows)

    def drain(c):
        first_kind = c % 2 == 1
        send_inc(c).wait_send()

        @pl.when(c % cuts == 0)
        def _():
            send_rows(c // cuts, upper).wait_send()

        for stream in (ZA, YA):
            for copy in send_code(stream, c):
                copy.wait_send()

        @pl.when(is_odd == first_kind)
        def _():
            for copy in send_code(ZB, c):
                copy.wait_send()

        @pl.when(is_even == first_kind)
        def _():
            for copy in send_code(YB, c):
                copy.wait_send()

    @pl.loop(0, pieces + LAGS[3])
    def _(t):
        @pl.when((t % cuts == 0) & (t < pieces))
        def _():
            first_hop(t // cuts)

        @pl.when((t >= LAGS[0]) & (t < pieces + LAGS[0]))
        def _():
            second_hop(t - LAGS[0])

        @pl.when((t >= LAGS[1]) & (t < pieces + LAGS[1]))
        def _():
            third_hop(t - LAGS[1])

        @pl.when(t == LAGS[1])
        def _():
            pairs = width // 2
            unordered = col * pairs + iota((pairs, 1), 0)
            values = pair_sum(vir_table[...], NV, unordered.astype(F32))
            same = iota((pairs, width), 1) // 2 == iota((pairs, width), 0)
            vir_row[...] = jnp.sum(jnp.where(same, values, 0.0), axis=0, keepdims=True)
            for j in range(row_count // CHUNK):
                rows = pl.ds(j * CHUNK, CHUNK)
                block = jnp.broadcast_to(slot_row[:, rows], (CHUNK, CHUNK))
                slot_col[rows, :] = block.T
            acc[...] = jnp.zeros_like(acc)

        @pl.when((t >= LAGS[2]) & (t < pieces + LAGS[2]))
        def _():
            finish(t - LAGS[2])

        @pl.when((t >= LAGS[3]) & ((t - LAGS[3]) % cuts == cuts - 1))
        def _():
            spread((t - LAGS[3]) // cuts)

        @pl.when(t >= LAGS[3])
        def _():
            drain(t - LAGS[3])


def shards(amplitudes, integrals, pair_index, partner, occ_energy, vir_energy):
    row_count, width = amplitudes.shape
    row_half = lax.axis_size("row") // 2
    col_count = lax.axis_size("col")
    chunks = row_count // 2 // CHUNK
    pieces = row_count // 2 // PIECE
    dma = pltpu.SemaphoreType.DMA
    return pl.pallas_call(
        functools.partial(kernel, chunks, width, row_half, col_count),
        out_shape=jax.ShapeDtypeStruct((row_count, width), BF16),
        in_specs=[pl.BlockSpec(memory_space=pltpu.HBM)] * 6,
        out_specs=pl.BlockSpec(memory_space=pltpu.VMEM),
        scratch_shapes=[
            pltpu.VMEM((row_count, CHUNK), jnp.int32),
            pltpu.VMEM((1, row_count), jnp.int32),
            pltpu.VMEM((1, row_count), jnp.int32),
            pltpu.VMEM((1, occ_energy.shape[0]), F32),
            pltpu.VMEM((1, vir_energy.shape[0]), F32),
            pltpu.VMEM((row_count, width), BF16),
            pltpu.VMEM((width, STOPS * width), BF16),
            pltpu.VMEM((width, STOPS * width), BF16),
            pltpu.VMEM((1, row_count), jnp.int32),
            pltpu.VMEM((1, row_count), F32),
            pltpu.VMEM((1, width), F32),
            pltpu.VMEM((chunks, CHUNK, width), BF16),
            pltpu.VMEM((2, chunks, CHUNK, width), BF16),
            pltpu.VMEM((STOPS, pieces, PIECE, width), F32),
            pltpu.VMEM((PIECE, width), F32),
            pltpu.VMEM((pieces, PIECE, 1), F32),
            pltpu.VMEM((4, pieces, PIECE, width), jnp.int16),
            pltpu.VMEM((4, pieces, PIECE, width), jnp.int16),
            pltpu.VMEM((4, pieces, 1, width), F32),
            pltpu.VMEM((4, pieces, 1, width), F32),
            pltpu.VMEM((pieces, PIECE, width), BF16),
            pltpu.VMEM((chunks, 2 * CHUNK, width), BF16),
            dma((5 + LOADS,)),
            dma((chunks,)),
            dma((chunks,)),
            dma((4, pieces)),
            dma((4, pieces)),
            dma((4, pieces)),
            dma((4, pieces)),
            dma((pieces,)),
            dma((pieces,)),
        ],
        compiler_params=pltpu.CompilerParams(
            collective_id=0, has_side_effects=True, vmem_limit_bytes=48 * 1024 * 1024
        ),
    )(
        pltpu.with_memory_space_constraint(amplitudes, pltpu.HBM),
        pltpu.with_memory_space_constraint(integrals, pltpu.HBM),
        pltpu.with_memory_space_constraint(partner[None, :], pltpu.HBM),
        pltpu.with_memory_space_constraint(pair_index[None, :], pltpu.HBM),
        pltpu.with_memory_space_constraint(occ_energy[None, :], pltpu.HBM),
        pltpu.with_memory_space_constraint(vir_energy[None, :], pltpu.HBM),
    )


def solution(mesh):
    in_specs = (P("row", "col"), P("col", None), P("row"), P("row"), P(), P())
    out_specs = P("row", "col")
    return jax.shard_map(shards, mesh=mesh, in_specs=in_specs, out_specs=out_specs, check_vma=False)
```

```python
import functools

import jax
import jax.numpy as jnp
from jax import lax
from jax.experimental import pallas as pl
from jax.experimental.pallas import tpu as pltpu
from jax.sharding import PartitionSpec as P

NOCC = 200
NV = 2000
STOPS = 4
CHUNK = 128
PIECE = 64
LOADS = 4
LAGS = (2, 5, 9, 14)
ZA, YA, ZB, YB = range(4)
LEVELS = 32767.0
MESH = pl.DeviceIdType.MESH
F32 = jnp.float32
BF16 = jnp.bfloat16


def iota(shape, dim):
    return lax.broadcasted_iota(jnp.int32, shape, dim)


def encode(values, code_ref, scale_ref):
    top = jnp.maximum(jnp.max(jnp.abs(values), axis=0, keepdims=True), 1e-30)
    code = jnp.round(values * (LEVELS / top))
    code_ref[...] = code.astype(jnp.int32).astype(jnp.int16)
    scale_ref[...] = top * (1.0 / LEVELS)


def decode(code_ref, scale_ref):
    return code_ref[...].astype(jnp.int32).astype(F32) * scale_ref[...]


def lookup(table, position):
    slots = iota((position.shape[0], table.shape[1]), 1).astype(F32)
    return jnp.sum(jnp.where(slots == position, table, 0.0), axis=1, keepdims=True)


def pair_sum(table, base, position):
    first = jnp.floor((position + 0.5) * (1.0 / base))
    return lookup(table, first) + lookup(table, position - first * base)


def place(slot_ref, inc, first, rows):
    at = slot_ref[rows, :]
    lane = iota(at.shape, 1)
    one_hot = jnp.where(at == lane + first, 1.0, 0.0).astype(BF16)
    return jnp.dot(one_hot, inc, preferred_element_type=F32).astype(BF16)


def kernel(
    chunks,
    width,
    row_half,
    col_count,
    amp_hbm,
    integ_hbm,
    partner_hbm,
    pair_hbm,
    occ_hbm,
    vir_hbm,
    acc,
    slot_col,
    partner_row,
    pair_row,
    occ_table,
    vir_table,
    amp,
    integ,
    mirror,
    slot_row,
    pair_f,
    vir_row,
    rows_send,
    rows_all,
    part,
    total,
    occ_chunk,
    code_send,
    code_recv,
    scale_send,
    scale_recv,
    inc_send,
    inc_all,
    load_sem,
    rows_ssem,
    rows_rsem,
    code_ssem,
    code_rsem,
    scale_ssem,
    scale_rsem,
    inc_ssem,
    inc_rsem,
):
    row = lax.axis_index("row")
    col = lax.axis_index("col")
    upper = row // row_half
    odd = col % 2
    mine = (upper + odd) % 2
    half = chunks * CHUNK
    cuts = CHUNK // PIECE
    pieces = chunks * cuts
    row_count = 2 * half
    partner = (row + row_half) % (2 * row_half)
    col_up = (col + 2) % col_count
    col_down = (col + col_count - 2) % col_count
    col_flip = col + 1 - 2 * odd

    part_rows = row_count // LOADS
    slices = [pl.ds(i * part_rows, part_rows) for i in range(LOADS)]
    moves = [(partner_hbm, partner_row)]
    moves += [(amp_hbm.at[rows], amp.at[rows]) for rows in slices]
    moves += [(pair_hbm, pair_row), (occ_hbm, occ_table), (vir_hbm, vir_table)]
    moves += [(integ_hbm, integ)]
    loads = [
        pltpu.make_async_copy(source, target, load_sem.at[i])
        for i, (source, target) in enumerate(moves)
    ]
    for load in loads[: 1 + LOADS]:
        load.start()

    barrier = pltpu.get_barrier_semaphore()
    for peer in ((partner, col), (partner, col_flip), (row, col_up), (row, col_down)):
        pl.semaphore_signal(barrier, inc=1, device_id=peer, device_id_type=MESH)

    def send_rows(c, slot):
        return pltpu.make_async_remote_copy(
            src_ref=rows_send.at[c],
            dst_ref=rows_all.at[slot, c],
            send_sem=rows_ssem.at[c],
            recv_sem=rows_rsem.at[c],
            device_id=(partner, col),
            device_id_type=MESH,
        )

    def send_code(stream, c):
        peer = (row, col_up) if stream in (ZA, ZB) else (partner, col_flip)
        data = pltpu.make_async_remote_copy(
            src_ref=code_send.at[stream, c],
            dst_ref=code_recv.at[stream, c],
            send_sem=code_ssem.at[stream, c],
            recv_sem=code_rsem.at[stream, c],
            device_id=peer,
            device_id_type=MESH,
        )
        scale = pltpu.make_async_remote_copy(
            src_ref=scale_send.at[stream, c],
            dst_ref=scale_recv.at[stream, c],
            send_sem=scale_ssem.at[stream, c],
            recv_sem=scale_rsem.at[stream, c],
            device_id=peer,
            device_id_type=MESH,
        )
        return scale, data

    def send_inc(c):
        return pltpu.make_async_remote_copy(
            src_ref=inc_send.at[c],
            dst_ref=inc_all.at[c // cuts, pl.ds(CHUNK + c % cuts * PIECE, PIECE)],
            send_sem=inc_ssem.at[c],
            recv_sem=inc_rsem.at[c],
            device_id=(partner, col),
            device_id_type=MESH,
        )

    def push(stream, c, values):
        encode(values, code_send.at[stream, c], scale_send.at[stream, c])
        for copy in send_code(stream, c):
            copy.start()

    def arrived(stream, c):
        for copy in send_code(stream, c):
            copy.wait_recv()
        return decode(code_recv.at[stream, c], scale_recv.at[stream, c])

    def picks(base):
        return slot_row[...] == base + iota((CHUNK, row_count), 0)

    def own_rows(choice):
        one_hot = jnp.where(choice, 1.0, 0.0).astype(BF16)
        return jnp.dot(one_hot, amp[...], preferred_element_type=F32).astype(BF16)

    loads[0].wait()
    slot_row[...] = jnp.where(
        iota((1, row_count), 1) * 0 + upper > 0,
        partner_row[...] - partner * row_count,
        iota((1, row_count), 1),
    )
    for load in loads[1 : 1 + LOADS]:
        load.wait()
    for load in loads[1 + LOADS :]:
        load.start()
    rows_send[0] = own_rows(picks((1 - mine) * half))
    pl.semaphore_wait(barrier, 4)
    send_rows(0, upper).start()

    @pl.loop(1, chunks)
    def _(c):
        rows_send[c] = own_rows(picks((1 - mine) * half + c * CHUNK))
        send_rows(c, upper).start()

    for load in loads[1 + LOADS :]:
        load.wait()
    tile = 256
    right = iota((tile, tile), 1)
    swap = jnp.where(iota((tile, tile), 0) == right + 1 - 2 * (right % 2), 1.0, 0.0).astype(BF16)
    for t in range(STOPS * width // tile):
        cols = pl.ds(t * tile, tile)
        mirror[:, cols] = jnp.dot(integ[:, cols], swap, preferred_element_type=F32).astype(BF16)
    pair_f[...] = pair_row[...].astype(F32)

    even_lane = iota((PIECE, width), 1) % 2 == 0
    is_even = odd == 0
    is_odd = odd == 1
    is_upper = iota((PIECE, width), 1) * 0 + upper > 0

    def first_hop(c):
        choice = picks(mine * half + c * CHUNK)
        rows_all[upper, c] = own_rows(choice)
        send_rows(c, 1 - upper).wait_recv()
        low = rows_all[0, c]
        high = rows_all[1, c]

        def multiply(s):
            cols = pl.ds(s * width, width)
            product = jnp.dot(low, integ[:, cols], preferred_element_type=F32) + jnp.dot(
                high, mirror[:, cols], preferred_element_type=F32
            )
            for p in range(cuts):
                part[s, c * cuts + p] = product[p * PIECE : (p + 1) * PIECE]

        def push_parts(stream, s, start):
            for p in range(start, cuts, 2):
                push(stream, c * cuts + p, part[s, c * cuts + p])

        multiply(3)

        @pl.when(is_odd)
        def _():
            for p in range(cuts):
                push(ZA, c * cuts + p, part[3, c * cuts + p])

        @pl.when(is_even)
        def _():
            push_parts(YA, 3, 1)

        multiply(1)

        @pl.when(is_even)
        def _():
            push_parts(YB, 1, 1)

        multiply(2)

        @pl.when(is_odd)
        def _():
            push_parts(YB, 2, 0)

        multiply(0)
        pair = jnp.sum(jnp.where(choice, pair_f[...], 0.0), axis=1, keepdims=True)
        occ = pair_sum(occ_table[...], NOCC, pair)
        for p in range(cuts):
            occ_chunk[c * cuts + p] = occ[p * PIECE : (p + 1) * PIECE]

    def second_hop(c):
        first_kind = c % 2 == 1

        @pl.when(is_odd)
        def _():
            push(YA, c, part[1, c] + arrived(ZA, c))

        @pl.when(is_odd & first_kind)
        def _():
            push(ZB, c, part[2, c] + arrived(YA, c))

        @pl.when(is_even & ~first_kind)
        def _():
            push(ZB, c, part[3, c] + arrived(YB, c))

    def third_hop(c):
        first_kind = c % 2 == 1

        @pl.when(is_even & ~first_kind)
        def _():
            push(YA, c, part[1, c] + arrived(ZB, c))

        @pl.when(is_even)
        def _():
            push(ZA, c, part[2, c] + arrived(YA, c))

    def finish(c):
        first_kind = c % 2 == 1

        @pl.when(is_even)
        def _():
            total[...] = part[0, c] + arrived(ZA, c)

        @pl.when(is_odd & first_kind)
        def _():
            total[...] = part[0, c] + arrived(ZB, c) + arrived(YB, c)

        @pl.when(is_odd & ~first_kind)
        def _():
            total[...] = part[0, c] + arrived(YA, c)

        plain = total[...] / (vir_row[...] - occ_chunk[c])
        mirrored = jnp.where(
            even_lane,
            pltpu.roll(plain, width - 1, axis=1),
            pltpu.roll(plain, 1, axis=1),
        )
        inc_send[c] = jnp.where(is_upper, plain, mirrored).astype(BF16)
        send_inc(c).start()
        inc_all[c // cuts, pl.ds(c % cuts * PIECE, PIECE)] = jnp.where(is_upper, mirrored, plain).astype(BF16)

    def spread(c, side):
        values = inc_all[c, pl.ds(side * CHUNK, CHUNK)]
        owner = mine if side == 0 else 1 - mine
        group = min(512, row_count)
        for j in range(row_count // group):
            rows = pl.ds(j * group, group)
            acc[rows, :] = acc[rows, :] + place(slot_col, values, owner * half + c * CHUNK, rows)

    def drain(c):
        first_kind = c % 2 == 1
        send_inc(c).wait_send()

        @pl.when(c % cuts == 0)
        def _():
            send_rows(c // cuts, upper).wait_send()

        for stream in (ZA, YA):
            for copy in send_code(stream, c):
                copy.wait_send()

        @pl.when(is_odd == first_kind)
        def _():
            for copy in send_code(ZB, c):
                copy.wait_send()

        @pl.when(is_even == first_kind)
        def _():
            for copy in send_code(YB, c):
                copy.wait_send()

    @pl.loop(0, pieces + LAGS[3])
    def _(t):
        @pl.when((t % cuts == 0) & (t < pieces))
        def _():
            first_hop(t // cuts)

        @pl.when((t >= LAGS[0]) & (t < pieces + LAGS[0]))
        def _():
            second_hop(t - LAGS[0])

        @pl.when((t >= LAGS[1]) & (t < pieces + LAGS[1]))
        def _():
            third_hop(t - LAGS[1])

        @pl.when(t == LAGS[1])
        def _():
            pairs = width // 2
            unordered = col * pairs + iota((pairs, 1), 0)
            values = pair_sum(vir_table[...], NV, unordered.astype(F32))
            same = iota((pairs, width), 1) // 2 == iota((pairs, width), 0)
            vir_row[...] = jnp.sum(jnp.where(same, values, 0.0), axis=0, keepdims=True)
            for j in range(row_count // CHUNK):
                rows = pl.ds(j * CHUNK, CHUNK)
                block = jnp.broadcast_to(slot_row[:, rows], (CHUNK, CHUNK))
                slot_col[rows, :] = block.T
            acc[...] = jnp.zeros_like(acc)

        @pl.when((t >= LAGS[2]) & (t < pieces + LAGS[2]))
        def _():
            finish(t - LAGS[2])

        @pl.when((t >= LAGS[2]) & (t < pieces + LAGS[2]) & ((t - LAGS[2]) % cuts == cuts - 1))
        def _():
            spread((t - LAGS[2]) // cuts, 0)

        @pl.when((t >= LAGS[3]) & ((t - LAGS[3]) % cuts == cuts - 1))
        def _():
            for p in range(cuts):
                send_inc((t - LAGS[3]) // cuts * cuts + p).wait_recv()
            spread((t - LAGS[3]) // cuts, 1)

        @pl.when(t >= LAGS[3])
        def _():
            drain(t - LAGS[3])


def shards(amplitudes, integrals, pair_index, partner, occ_energy, vir_energy):
    row_count, width = amplitudes.shape
    row_half = lax.axis_size("row") // 2
    col_count = lax.axis_size("col")
    chunks = row_count // 2 // CHUNK
    pieces = row_count // 2 // PIECE
    dma = pltpu.SemaphoreType.DMA
    return pl.pallas_call(
        functools.partial(kernel, chunks, width, row_half, col_count),
        out_shape=jax.ShapeDtypeStruct((row_count, width), BF16),
        in_specs=[pl.BlockSpec(memory_space=pltpu.HBM)] * 6,
        out_specs=pl.BlockSpec(memory_space=pltpu.VMEM),
        scratch_shapes=[
            pltpu.VMEM((row_count, CHUNK), jnp.int32),
            pltpu.VMEM((1, row_count), jnp.int32),
            pltpu.VMEM((1, row_count), jnp.int32),
            pltpu.VMEM((1, occ_energy.shape[0]), F32),
            pltpu.VMEM((1, vir_energy.shape[0]), F32),
            pltpu.VMEM((row_count, width), BF16),
            pltpu.VMEM((width, STOPS * width), BF16),
            pltpu.VMEM((width, STOPS * width), BF16),
            pltpu.VMEM((1, row_count), jnp.int32),
            pltpu.VMEM((1, row_count), F32),
            pltpu.VMEM((1, width), F32),
            pltpu.VMEM((chunks, CHUNK, width), BF16),
            pltpu.VMEM((2, chunks, CHUNK, width), BF16),
            pltpu.VMEM((STOPS, pieces, PIECE, width), F32),
            pltpu.VMEM((PIECE, width), F32),
            pltpu.VMEM((pieces, PIECE, 1), F32),
            pltpu.VMEM((4, pieces, PIECE, width), jnp.int16),
            pltpu.VMEM((4, pieces, PIECE, width), jnp.int16),
            pltpu.VMEM((4, pieces, 1, width), F32),
            pltpu.VMEM((4, pieces, 1, width), F32),
            pltpu.VMEM((pieces, PIECE, width), BF16),
            pltpu.VMEM((chunks, 2 * CHUNK, width), BF16),
            dma((5 + LOADS,)),
            dma((chunks,)),
            dma((chunks,)),
            dma((4, pieces)),
            dma((4, pieces)),
            dma((4, pieces)),
            dma((4, pieces)),
            dma((pieces,)),
            dma((pieces,)),
        ],
        compiler_params=pltpu.CompilerParams(
            collective_id=0, has_side_effects=True, vmem_limit_bytes=48 * 1024 * 1024
        ),
    )(
        pltpu.with_memory_space_constraint(amplitudes, pltpu.HBM),
        pltpu.with_memory_space_constraint(integrals, pltpu.HBM),
        pltpu.with_memory_space_constraint(partner[None, :], pltpu.HBM),
        pltpu.with_memory_space_constraint(pair_index[None, :], pltpu.HBM),
        pltpu.with_memory_space_constraint(occ_energy[None, :], pltpu.HBM),
        pltpu.with_memory_space_constraint(vir_energy[None, :], pltpu.HBM),
    )


def solution(mesh):
    in_specs = (P("row", "col"), P("col", None), P("row"), P("row"), P(), P())
    out_specs = P("row", "col")
    return jax.shard_map(shards, mesh=mesh, in_specs=in_specs, out_specs=out_specs, check_vma=False)
```
